32 devices in a mesh: dp: 4 (over z), ctx: 8 (over y, x, core).
Axes of the slice: x: 2, y: 2, z: 4, core: 2. Of those that a mesh axis runs over, the one named last changes fastest.
Arguments:
- tokens: bfloat16 [4, 1024, 8192], P('dp', 'ctx'), may hold values from -6 to 6
- w_down: bfloat16 [8192, 512], P(('dp', 'ctx')), may hold values from -0.0625 to 0.0625
- w_up: bfloat16 [512, 1024], replicated, may hold values from -0.25 to 0.25
- queries: bfloat16 [4, 1024, 4096], P('dp', 'ctx'), may hold values from -70 to 70, as said below
- block_order: int32 [4, 16], P('dp', 'ctx'), may hold values from 0 to 15, each once within a row
Outputs:
- attended: bfloat16 [4, 1024, 4096], P('dp', 'ctx')
The draws below stay inside these ranges and needn't reach their ends.
Inputs may be any that keep to these rules, and one draw needn't show every extreme that they name: `queries`: query entries.
All inputs are finite; a program needn't handle non-finite values.
Results may differ from the reference program's by a relative error of at most 0.014.
The reference program's roundings to bfloat16 on the way count: a program that leaves them out, or rounds other values in their place, can miss the bound.
Values may be sent and summed in bfloat16 or wider, within the bound.
A program may use at most 64 MiB of HBM per device.

```python
import jax
import jax.numpy as jnp
from jax import lax

D = 8192
R = 512
QH = 32
KVH = 4
HD = 128
HALF = 64
SEQ = 1024
N_DP = 4
N_CTX = 8


def draw_queries(key, part):
    shape = (N_DP, SEQ, QH * HD)
    return jnp.clip(jax.random.normal(key, shape, jnp.float32), -6.0, 6.0).astype(jnp.bfloat16)


def shard_levels(key, extent, pieces, least, high):
    loudness = 1.0
    for dim, parts in pieces:
        heights = jax.random.uniform(jax.random.fold_in(jax.random.fold_in(key, 6), dim), (parts,), jnp.float32, least / len(pieces), high / len(pieces))
        loudness = loudness * jnp.repeat(jnp.exp(heights), extent[dim] // parts).reshape((-1,) + (1,) * (len(extent) - 1 - dim))
    return loudness


def gaussian(rng, dims, width, most, cuts=(), kind=jnp.bfloat16):
    gain = shard_levels(rng, dims, cuts, -0.22, 0.18) if cuts else 1.0
    array = jax.random.normal(rng, dims, jnp.float32) * width * gain
    return jnp.minimum(jnp.maximum(array, -most), most).astype(kind)


def setup_inputs(seed: int = 0) -> dict:
    seeds = jax.random.split(jax.random.key(seed), 6)
    tokens = gaussian(seeds[0], (N_DP, SEQ, D), 1.0, 6.0, ((0, 4), (1, 8)))
    w_down = gaussian(seeds[1], (D, R), D ** -0.5, 0.0625, ((0, 32),))
    w_up = gaussian(seeds[2], (R, 2 * KVH * HD), R ** -0.5, 0.25)
    queries = draw_queries(jax.random.fold_in(seeds[5], 71), 0)
    block_order = jax.vmap(lambda own: jax.random.permutation(own, 2 * N_CTX))(jax.random.split(seeds[4], N_DP)).reshape((N_DP, 2 * N_CTX)).astype(jnp.int32)
    return dict(tokens=tokens, w_down=w_down, w_up=w_up, queries=queries, block_order=block_order)


def one_sequence(tokens_one, queries_one, order_one, w_down, w_up):
    latent = jnp.dot(tokens_one, w_down, preferred_element_type=jnp.float32).astype(jnp.bfloat16)
    kv_rows = jnp.dot(latent, w_up, preferred_element_type=jnp.float32).astype(jnp.bfloat16)
    row_ids = jnp.arange(SEQ, dtype=jnp.int32)
    position = jnp.take(order_one, row_ids // HALF).astype(jnp.int32) * HALF + row_ids % HALF
    key_heads = kv_rows[:, :KVH * HD].reshape(SEQ, KVH, HD).transpose(1, 0, 2)
    value_heads = kv_rows[:, KVH * HD:].reshape(SEQ, KVH, HD).transpose(1, 0, 2)
    query_heads = queries_one.reshape(SEQ, QH, HD).transpose(1, 0, 2)
    allowed = position[None, :] <= position[:, None]
    group = QH // KVH
    score_scale = HD ** -0.5

    def head(index):
        kv_index = index // group
        scores = jnp.dot(query_heads[index], key_heads[kv_index].T, preferred_element_type=jnp.float32) * score_scale
        scores = jnp.where(allowed, scores, -1e30)
        largest = jnp.max(scores, axis=1)
        expo = jnp.where(allowed, jnp.exp(scores - largest[:, None]), 0.0)
        total = jnp.sum(expo, axis=1)
        summed = jnp.dot(expo.astype(jnp.bfloat16), value_heads[kv_index], preferred_element_type=jnp.float32)
        return summed / total[:, None]

    outputs = lax.map(head, jnp.arange(QH, dtype=jnp.int32))
    return outputs.transpose(1, 0, 2).reshape(SEQ, QH * HD).astype(jnp.bfloat16)


def reference(tokens, w_down, w_up, queries, block_order):
    def single(args):
        return one_sequence(args[0], args[1], args[2], w_down, w_up)
    return lax.map(single, (tokens, queries, block_order))
```

```python
import functools
import math

import jax
import jax.numpy as jnp
from jax import lax
from jax.experimental import pallas as pl
from jax.experimental.pallas import tpu as pltpu
from jax.sharding import PartitionSpec as P

QH = 32
KVH = 4
HD = 128
MESH = pl.DeviceIdType.MESH


def attention_kernel(order_ref, pos_ref, latent_ref, w_up_ref, q_ref, out_ref, kv, bias):
    rows = q_ref.shape[1]
    count = latent_ref.shape[0]
    half = rows // 2
    tile = math.gcd(count, 256)

    @pl.loop(0, count // tile)
    def _(i):
        part = pl.ds(pl.multiple_of(i * tile, tile), tile)
        kv[part, :] = jnp.dot(
            latent_ref[part, :], w_up_ref[...], preferred_element_type=jnp.float32
        ).astype(jnp.bfloat16)

    ids = lax.broadcasted_iota(jnp.int32, (rows, 1), 0)
    query_pos = jnp.where(ids < half, order_ref[0, 0], order_ref[0, 1]) * half + ids % half
    bias[...] = jnp.where(pos_ref[0:1, :] <= query_pos, 0.0, -1e30)
    scale = HD ** (-0.5) * math.log2(math.e)
    heads = 2
    group = QH // KVH

    def step(i):
        def cols(first, width):
            return pl.ds(pl.multiple_of(first * HD, HD), width * HD)

        g = i * heads // group
        queries = jnp.concatenate(
            [q_ref[0, :, cols(i * heads + k, 1)] for k in range(heads)], axis=0
        )
        scores = lax.dot_general(
            queries, kv[:, cols(g, 1)], (((1,), (1,)), ((), ())), preferred_element_type=jnp.float32
        )
        parts, totals = [], []
        for k in range(heads):
            kept = scores[k * rows : (k + 1) * rows] * scale + bias[...]
            largest = jnp.max(kept, axis=1, keepdims=True)
            expo = jnp.exp2(kept - largest)
            totals.append(jnp.sum(expo, axis=1, keepdims=True))
            parts.append(expo.astype(jnp.bfloat16))
        summed = jnp.dot(
            jnp.concatenate(parts, axis=0), kv[:, cols(KVH + g, 1)], preferred_element_type=jnp.float32
        )
        for k in range(heads):
            out_ref[0, :, cols(i * heads + k, 1)] = (
                summed[k * rows : (k + 1) * rows] / totals[k]
            ).astype(jnp.bfloat16)

    pairs = QH // heads
    together = 4 if count <= 1024 else 1

    @pl.loop(0, pairs // together)
    def _(i):
        for k in range(together):
            step(i * together + k)


def attend(block_order, positions, latent, w_up, queries):
    count = latent.shape[0]
    rows = queries.shape[1]
    vmem = pl.BlockSpec(memory_space=pltpu.VMEM)
    return pl.pallas_call(
        attention_kernel,
        out_shape=jax.ShapeDtypeStruct(queries.shape, jnp.bfloat16),
        in_specs=[pl.BlockSpec(memory_space=pltpu.SMEM), vmem, vmem, vmem, vmem],
        out_specs=vmem,
        scratch_shapes=[
            pltpu.VMEM((count, w_up.shape[1]), jnp.bfloat16),
            pltpu.VMEM((rows, count), jnp.float32),
        ],
        compiler_params=pltpu.CompilerParams(vmem_limit_bytes=48 * 2**20),
        name="attention",
    )(block_order, positions, latent, w_up, queries)


def latent_kernel(
    layers, order_ref, tokens_ref, w_ref, latent_ref, pos_ref,
    tok, w, acc, share, mine, gathered, pos_mine, pos_all,
    load_sem, own_sem, tok_send, tok_recv, w_send, w_recv, piece_recv,
    pos_send, pos_recv, sum_sem, lat_send, lat_recv, store_sem,
):
    plane = 8
    z, ctx = lax.axis_index("dp"), lax.axis_index("ctx")
    core, x, y = ctx % 2, ctx // 2 % 2, ctx // 4
    mate = ctx + 1 - 2 * core
    x_dev, y_dev = ctx + 2 - 4 * x, ctx + 4 - 8 * y
    p, px, py = y * 2 + x, y * 2 + 1 - x, (1 - y) * 2 + x
    pd = (1 - y) * 2 + 1 - x
    rows, depth, width = tokens_ref.shape[1], w_ref.shape[0], w_ref.shape[1]
    chunks = layers * 4
    quarter = depth // 4
    own = z * 4 + p

    def columns(j, side):
        return pl.ds(pl.multiple_of((j * 2 + side) * depth, depth), depth)

    def load(j):
        return pltpu.make_async_copy(
            tokens_ref.at[0, :, columns(j, core)], tok.at[j, pl.ds(0, rows), :], load_sem.at[j]
        )

    def swap(j):
        return pltpu.make_async_remote_copy(
            tokens_ref.at[0, :, columns(j, 1 - core)], tok.at[j, pl.ds(rows, rows), :],
            tok_send.at[j], tok_recv.at[j], device_id=(z, mate), device_id_type=MESH,
        )

    own_load = pltpu.make_async_copy(w_ref, w.at[own], own_sem)
    own_load.start()

    barrier = pltpu.get_barrier_semaphore()
    for d in range(1, plane):
        pl.semaphore_signal(barrier, inc=1, device_id=(z, (ctx + d) % plane), device_id_type=MESH)

    @pl.when(z > 0)
    def _():
        pl.semaphore_signal(barrier, inc=1, device_id=(z - 1, ctx), device_id_type=MESH)

    @pl.when(z < layers - 1)
    def _():
        pl.semaphore_signal(barrier, inc=1, device_id=(z + 1, ctx), device_id_type=MESH)

    edge = layers - 1
    along = (z + edge - 1) // edge + (edge - z + edge - 1) // edge
    pl.semaphore_wait(barrier, plane - 1 + along)

    sent = []

    def send(conds, src, dst, sem, device):
        index = len(sent)

        def copy():
            return pltpu.make_async_remote_copy(
                src, dst, w_send.at[index], sem, device_id=device, device_id_type=MESH
            )

        sent.append((conds, copy))
        when(conds, lambda: copy().start())

    def when(conds, body):
        if not conds:
            body()
        elif len(conds) == 1:
            pl.when(conds[0])(body)
        else:
            pl.when(jnp.logical_and(conds[0], conds[1]))(body)

    def arrived(dst, sem):
        pltpu.make_async_remote_copy(
            dst, dst, w_send.at[0], sem, device_id=(z, mate), device_id_type=MESH
        ).wait_recv()

    def multiply(j):
        acc[...] += jnp.dot(tok[j], w[j], preferred_element_type=jnp.float32)

    def inside(layer):
        return jnp.logical_and(layer >= 0, layer < layers)

    def sources(t):
        if t == 0:
            return [(0, z, [])]
        return [(s, z + s * t, [inside(z + s * t)]) for s in (-1, 1)]

    def ahead(s):
        return [1, -1] if s == 0 else [-s]

    def piece(j, q):
        return w.at[j, pl.ds(q * quarter, quarter), :]

    def column(t):
        for s, layer, conds in sources(t):
            j = layer * 4 + p
            block = w_ref if t == 0 else w.at[j]
            if t:
                when(conds, lambda: arrived(w.at[j], w_recv.at[j]))
            for step in ahead(s):
                send(conds + [inside(z + step)], block, w.at[j], w_recv.at[j], (z + step, ctx))
            send(conds, block, w.at[j], w_recv.at[j], (z, x_dev))
            send(conds, block, w.at[j], w_recv.at[j], (z, y_dev))
            if t:
                when(conds, lambda: multiply(j))

    def sides(t):
        for s, layer, conds in sources(t):
            for place, device, first in ((px, y_dev, 0), (py, x_dev, 1)):
                j = layer * 4 + place
                when(conds, lambda: arrived(w.at[j], w_recv.at[j]))
                for q in (first + 2, first) if t == 0 else (first,):
                    send(conds, piece(j, q), piece(j, q), piece_recv.at[layer, q], (z, device))
            for place in (px, py):
                when(conds, lambda: multiply(layer * 4 + place))

    def corner(t):
        for s, layer, conds in sources(t):
            j = layer * 4 + pd
            for q in (2, 3):
                when(conds, lambda: arrived(piece(j, q), piece_recv.at[layer, q]))
                for step in ahead(s):
                    send(
                        conds + [inside(z + step)], piece(j, q), piece(j, q), piece_recv.at[layer, q],
                        (z + step, ctx),
                    )
            for q in (0, 1):
                when(conds, lambda: arrived(piece(j, q), piece_recv.at[layer, q]))
            when(conds, lambda: multiply(j))

    column(0)

    def start_tokens(j, unused):
        swap(j).start()
        load(j).start()
        return unused

    lax.fori_loop(0, chunks, start_tokens, 0)

    half = rows // 2
    ids = lax.broadcasted_iota(jnp.int32, (8, rows), 1)
    pos_mine[...] = jnp.where(ids < half, order_ref[0, 0], order_ref[0, 1]) * half + ids % half

    def pos_slot(device):
        return pos_all.at[:, pl.ds(pl.multiple_of(device * rows, rows), rows)]

    def pos_copy(d):
        return pltpu.make_async_remote_copy(
            pos_mine, pos_slot(ctx), pos_send.at[d], pos_recv.at[ctx],
            device_id=(z, (ctx + d) % plane), device_id_type=MESH,
        )

    for d in range(1, plane):
        pos_copy(d).start()
    pos_all[:, pl.ds(pl.multiple_of(ctx * rows, rows), rows)] = pos_mine[...]

    def wait_tokens(j, unused):
        load(j).wait()
        swap(j).wait()
        return unused

    lax.fori_loop(0, chunks, wait_tokens, 0)
    own_load.wait()
    acc[...] = jnp.dot(tok[own], w[own], preferred_element_type=jnp.float32)

    for t in range(layers + 2):
        if 1 <= t < layers:
            column(t)
        if 0 <= t - 1 < layers:
            sides(t - 1)
        if 0 <= t - 2 < layers:
            corner(t - 2)

    total = pltpu.make_async_remote_copy(
        acc.at[pl.ds(rows, rows), :], share, sum_sem.at[0], sum_sem.at[1],
        device_id=(z, mate), device_id_type=MESH,
    )
    total.start()
    for conds, copy in sent:
        when(conds, lambda: copy().wait_send())
    for d in range(1, plane):
        pos_copy(d).wait_send()
        sender = (ctx + d) % plane
        pltpu.make_async_remote_copy(
            pos_mine, pos_slot(sender), pos_send.at[d], pos_recv.at[sender],
            device_id=(z, mate), device_id_type=MESH,
        ).wait_recv()
    pos_store = pltpu.make_async_copy(pos_all, pos_ref, store_sem.at[plane])
    pos_store.start()
    total.wait()
    mine[...] = (acc[0:rows, :] + share[...]).astype(jnp.bfloat16)

    part = rows // 2

    def block(device, first=0, size=rows):
        return gathered.at[pl.ds(pl.multiple_of(device * rows + first, part), size), :]

    lat_sent = []

    def lat_send_to(src, dst, recv, device):
        copy = pltpu.make_async_remote_copy(
            src, dst, lat_send.at[len(lat_sent)], lat_recv.at[recv], device_id=(z, device), device_id_type=MESH
        )
        copy.start()
        lat_sent.append(copy)

    def lat_arrived(dst, recv):
        pltpu.make_async_remote_copy(
            dst, dst, lat_send.at[0], lat_recv.at[recv], device_id=(z, mate), device_id_type=MESH
        ).wait_recv()

    stores = []

    def store(src, device, index):
        copy = pltpu.make_async_copy(
            src, latent_ref.at[pl.ds(pl.multiple_of(device * rows, rows), rows), :], store_sem.at[index]
        )
        copy.start()
        stores.append(copy)

    def partner(device):
        return device + 1 - 2 * core

    d_dev = pd * 2 + core
    lat_send_to(mine, block(ctx), 0, x_dev)
    lat_send_to(mine, block(ctx), 1, y_dev)
    lat_send_to(mine, block(ctx), 2, mate)
    store(mine, ctx, 0)
    lat_arrived(block(x_dev), 0)
    lat_send_to(block(x_dev, 0, part), block(x_dev, 0, part), 3, y_dev)
    lat_send_to(block(x_dev), block(x_dev), 5, mate)
    store(block(x_dev), x_dev, 1)
    lat_arrived(block(y_dev), 1)
    lat_send_to(block(y_dev, part, part), block(y_dev, part, part), 4, x_dev)
    lat_send_to(block(y_dev), block(y_dev), 6, mate)
    store(block(y_dev), y_dev, 2)
    lat_arrived(block(mate), 2)
    store(block(mate), mate, 3)
    lat_arrived(block(d_dev, 0, part), 3)
    lat_send_to(block(d_dev, 0, part), block(d_dev, 0, part), 7, mate)
    lat_arrived(block(d_dev, part, part), 4)
    lat_send_to(block(d_dev, part, part), block(d_dev, part, part), 8, mate)
    store(block(d_dev), d_dev, 4)
    lat_arrived(block(partner(x_dev)), 5)
    store(block(partner(x_dev)), partner(x_dev), 5)
    lat_arrived(block(partner(y_dev)), 6)
    store(block(partner(y_dev)), partner(y_dev), 6)
    lat_arrived(block(partner(d_dev), 0, part), 7)
    lat_arrived(block(partner(d_dev), part, part), 8)
    store(block(partner(d_dev)), partner(d_dev), 7)
    for copy in lat_sent:
        copy.wait_send()
    for copy in stores:
        copy.wait()
    pos_store.wait()


def gather_latent(layers, tokens, w_down, block_order):
    rows, features = tokens.shape[1], tokens.shape[2]
    depth, width = w_down.shape
    chunks = layers * 4
    dma = pltpu.SemaphoreType.DMA
    whole = pl.BlockSpec(memory_space=pl.ANY)
    return pl.pallas_call(
        functools.partial(latent_kernel, layers),
        out_shape=[
            jax.ShapeDtypeStruct((8 * rows, width), jnp.bfloat16),
            jax.ShapeDtypeStruct((8, 8 * rows), jnp.int32),
        ],
        in_specs=[pl.BlockSpec(memory_space=pltpu.SMEM), whole, whole],
        out_specs=[whole, whole],
        scratch_shapes=[
            pltpu.VMEM((chunks, 2 * rows, depth), jnp.bfloat16),
            pltpu.VMEM((chunks, depth, width), jnp.bfloat16),
            pltpu.VMEM((2 * rows, width), jnp.float32),
            pltpu.VMEM((rows, width), jnp.float32),
            pltpu.VMEM((rows, width), jnp.bfloat16),
            pltpu.VMEM((8 * rows, width), jnp.bfloat16),
            pltpu.VMEM((8, rows), jnp.int32),
            pltpu.VMEM((8, 8 * rows), jnp.int32),
            dma((chunks,)),
            dma,
            dma((chunks,)),
            dma((chunks,)),
            dma((96,)),
            dma((chunks,)),
            dma((layers, 4)),
            dma((8,)),
            dma((8,)),
            dma((2,)),
            dma((10,)),
            dma((9,)),
            dma((9,)),
        ],
        compiler_params=pltpu.CompilerParams(
            collective_id=0, has_side_effects=True, vmem_limit_bytes=48 * 2**20
        ),
        name="latent",
    )(block_order, tokens, w_down)


def per_device(layers, plane, tokens, w_down, w_up, queries, block_order):
    local_rows = tokens.shape[1]
    half_rows = local_rows // 2
    if plane == 8:
        latent, positions = gather_latent(layers, tokens, w_down, block_order)
        return attend(block_order, positions, latent, w_up, queries)
    summed = jnp.dot(
        tokens[0],
        lax.all_gather(w_down, ("dp", "ctx"), axis=0, tiled=True),
        preferred_element_type=jnp.float32,
    )
    latent = lax.all_gather(summed.astype(jnp.bfloat16), "ctx", axis=0, tiled=True)
    order = lax.all_gather(block_order, "ctx", axis=1, tiled=True)
    positions = jnp.repeat(order, half_rows, axis=1) * half_rows + jnp.tile(
        jnp.arange(half_rows, dtype=jnp.int32), order.shape[1]
    )
    return attend(block_order, positions, latent, w_up, queries)


def solution(mesh):
    placed = (
        P("dp", "ctx", None),
        P(("dp", "ctx"), None),
        P(),
        P("dp", "ctx", None),
        P("dp", "ctx"),
    )
    sizes = mesh.shape["dp"], mesh.shape["ctx"]
    return jax.shard_map(
        functools.partial(per_device, *sizes), mesh=mesh, in_specs=placed, out_specs=P("dp", "ctx", None), check_vma=False
    )
```

```python
import functools
import math

import jax
import jax.numpy as jnp
from jax import lax
from jax.experimental import pallas as pl
from jax.experimental.pallas import tpu as pltpu
from jax.sharding import PartitionSpec as P

QH = 32
KVH = 4
HD = 128
MESH = pl.DeviceIdType.MESH


def attention_kernel(order_ref, pos_ref, latent_ref, w_up_ref, q_ref, out_ref, kv, bias):
    rows = q_ref.shape[1]
    count = latent_ref.shape[0]
    half = rows // 2
    tile = math.gcd(count, 256)

    @pl.loop(0, count // tile)
    def _(i):
        part = pl.ds(pl.multiple_of(i * tile, tile), tile)
        kv[part, :] = jnp.dot(
            latent_ref[part, :], w_up_ref[...], preferred_element_type=jnp.float32
        ).astype(jnp.bfloat16)

    ids = lax.broadcasted_iota(jnp.int32, (rows, 1), 0)
    query_pos = jnp.where(ids < half, order_ref[0, 0], order_ref[0, 1]) * half + ids % half
    bias[...] = jnp.where(pos_ref[0:1, :] <= query_pos, 0.0, -1e30)
    scale = HD ** (-0.5) * math.log2(math.e)
    heads = 2
    group = QH // KVH

    def step(i):
        def cols(first, width):
            return pl.ds(pl.multiple_of(first * HD, HD), width * HD)

        g = i * heads // group
        queries = jnp.concatenate(
            [q_ref[0, :, cols(i * heads + k, 1)] for k in range(heads)], axis=0
        )
        scores = lax.dot_general(
            queries, kv[:, cols(g, 1)], (((1,), (1,)), ((), ())), preferred_element_type=jnp.float32
        )
        parts, totals = [], []
        for k in range(heads):
            kept = scores[k * rows : (k + 1) * rows] * scale + bias[...]
            largest = jnp.max(kept, axis=1, keepdims=True)
            expo = jnp.exp2(kept - largest)
            totals.append(jnp.sum(expo, axis=1, keepdims=True))
            parts.append(expo.astype(jnp.bfloat16))
        summed = jnp.dot(
            jnp.concatenate(parts, axis=0), kv[:, cols(KVH + g, 1)], preferred_element_type=jnp.float32
        )
        for k in range(heads):
            out_ref[0, :, cols(i * heads + k, 1)] = (
                summed[k * rows : (k + 1) * rows] / totals[k]
            ).astype(jnp.bfloat16)

    pairs = QH // heads
    together = 4 if count <= 1024 else 1

    @pl.loop(0, pairs // together)
    def _(i):
        for k in range(together):
            step(i * together + k)


def attend(block_order, positions, latent, w_up, queries):
    count = latent.shape[0]
    rows = queries.shape[1]
    vmem = pl.BlockSpec(memory_space=pltpu.VMEM)
    return pl.pallas_call(
        attention_kernel,
        out_shape=jax.ShapeDtypeStruct(queries.shape, jnp.bfloat16),
        in_specs=[pl.BlockSpec(memory_space=pltpu.SMEM), vmem, vmem, vmem, vmem],
        out_specs=vmem,
        scratch_shapes=[
            pltpu.VMEM((count, w_up.shape[1]), jnp.bfloat16),
            pltpu.VMEM((rows, count), jnp.float32),
        ],
        compiler_params=pltpu.CompilerParams(vmem_limit_bytes=48 * 2**20),
        name="attention",
    )(block_order, positions, latent, w_up, queries)


def order(layers):
    steps = [("a", 0, 0), ("c", 1, 0), ("a", 0, 1), ("c", 1, 1), ("z", 0, 0), ("z", 0, 1)]
    for t in range(1, layers):
        if t + 1 < layers:
            steps += [("c", t + 1, 0), ("c", t + 1, 1)]
        if t > 1:
            steps += [("z", t - 1, 0), ("z", t - 1, 1), ("A", t - 2)]
        steps += [("C", t), ("a", t, 0), ("a", t, 1)]
    steps += [("Z", t) for t in range(layers - 2)] + [("A", layers - 2)]
    steps += [("z", layers - 1, 0), ("z", layers - 1, 1), ("A", layers - 1), ("Z", layers - 2), ("Z", layers - 1)]
    return steps


def latent_kernel(
    layers, order_ref, tokens_ref, w_ref, latent_ref, pos_ref,
    tok, w, acc, share, mine, gathered, pos_mine, pos_all,
    load_sem, own_sem, tok_send, tok_recv, w_send, w_recv, piece_recv,
    pos_send, pos_recv, sum_sem, lat_send, lat_recv, store_sem,
):
    plane = 8
    z, ctx = lax.axis_index("dp"), lax.axis_index("ctx")
    core, x, y = ctx % 2, ctx // 2 % 2, ctx // 4
    mate = ctx + 1 - 2 * core
    x_dev, y_dev = ctx + 2 - 4 * x, ctx + 4 - 8 * y
    p, px, py = y * 2 + x, y * 2 + 1 - x, (1 - y) * 2 + x
    pd = (1 - y) * 2 + 1 - x
    rows, depth, width = tokens_ref.shape[1], w_ref.shape[0], w_ref.shape[1]
    chunks = layers * 4
    quarter = depth // 4
    own = z * 4 + p

    def columns(j, side):
        return pl.ds(pl.multiple_of((j * 2 + side) * depth, depth), depth)

    def load(j):
        return pltpu.make_async_copy(
            tokens_ref.at[0, :, columns(j, core)], tok.at[j, pl.ds(0, rows), :], load_sem.at[j]
        )

    def swap(j):
        return pltpu.make_async_remote_copy(
            tokens_ref.at[0, :, columns(j, 1 - core)], tok.at[j, pl.ds(rows, rows), :],
            tok_send.at[j], tok_recv.at[j], device_id=(z, mate), device_id_type=MESH,
        )

    own_load = pltpu.make_async_copy(w_ref, w.at[own], own_sem)
    own_load.start()

    barrier = pltpu.get_barrier_semaphore()
    for d in range(1, plane):
        pl.semaphore_signal(barrier, inc=1, device_id=(z, (ctx + d) % plane), device_id_type=MESH)

    @pl.when(z > 0)
    def _():
        pl.semaphore_signal(barrier, inc=1, device_id=(z - 1, ctx), device_id_type=MESH)

    @pl.when(z < layers - 1)
    def _():
        pl.semaphore_signal(barrier, inc=1, device_id=(z + 1, ctx), device_id_type=MESH)

    edge = layers - 1
    along = (z + edge - 1) // edge + (edge - z + edge - 1) // edge
    pl.semaphore_wait(barrier, plane - 1 + along)

    sent = []

    def send(conds, src, dst, sem, device):
        index = len(sent)

        def copy():
            return pltpu.make_async_remote_copy(
                src, dst, w_send.at[index], sem, device_id=device, device_id_type=MESH
            )

        sent.append((conds, copy))
        when(conds, lambda: copy().start())

    def when(conds, body):
        if not conds:
            body()
        elif len(conds) == 1:
            pl.when(conds[0])(body)
        else:
            pl.when(jnp.logical_and(conds[0], conds[1]))(body)

    def arrived(dst, sem):
        pltpu.make_async_remote_copy(
            dst, dst, w_send.at[0], sem, device_id=(z, mate), device_id_type=MESH
        ).wait_recv()

    def multiply(j):
        acc[...] += jnp.dot(tok[j], w[j], preferred_element_type=jnp.float32)

    def inside(layer):
        return jnp.logical_and(layer >= 0, layer < layers)

    def sources(t):
        if t == 0:
            return [(0, z, [])]
        return [(s, z + s * t, [inside(z + s * t)]) for s in (-1, 1)]

    def ahead(s):
        return [1, -1] if s == 0 else [-s]

    def piece(j, q):
        return w.at[j, pl.ds(q * quarter, quarter), :]

    def side(j, h):
        return w.at[j, pl.ds(h * 2 * quarter, 2 * quarter), :]

    def column(t, h):
        for s, layer, conds in sources(t):
            j = layer * 4 + p
            block = w_ref.at[pl.ds(h * 2 * quarter, 2 * quarter), :] if t == 0 else side(j, h)
            if t:
                when(conds, lambda: arrived(side(j, h), w_recv.at[j, h]))
            for step in ahead(s):
                send(conds + [inside(z + step)], block, side(j, h), w_recv.at[j, h], (z + step, ctx))
            for device in (x_dev, y_dev):
                send(conds, block, side(j, h), w_recv.at[j, h], (z, device))

    def across(t, h):
        place, device = ((px, y_dev), (py, x_dev))[h]
        for s, layer, conds in sources(t):
            j = layer * 4 + place
            when(conds, lambda: arrived(side(j, h), w_recv.at[j, h]))
            for q in (2 * h + 1, 2 * h) if t == 0 else (2 * h,):
                send(conds, piece(j, q), piece(j, q), piece_recv.at[layer, q], (z, device))

    def corner(t, h):
        q = 2 * h + 1
        for s, layer, conds in sources(t):
            j = layer * 4 + pd
            when(conds, lambda: arrived(piece(j, q), piece_recv.at[layer, q]))
            for step in ahead(s):
                send(
                    conds + [inside(z + step)], piece(j, q), piece(j, q), piece_recv.at[layer, q], (z + step, ctx)
                )

    def finish_column(t):
        for s, layer, conds in sources(t):
            when(conds, lambda: multiply(layer * 4 + p))

    def finish_across(t):
        for s, layer, conds in sources(t):
            for place, h in ((px, 1), (py, 0)):
                j = layer * 4 + place
                when(conds, lambda: arrived(side(j, h), w_recv.at[j, h]))
            for place in (px, py):
                when(conds, lambda: multiply(layer * 4 + place))

    def finish_corner(t):
        for s, layer, conds in sources(t):
            j = layer * 4 + pd
            for q in (0, 2):
                when(conds, lambda: arrived(piece(j, q), piece_recv.at[layer, q]))
            when(conds, lambda: multiply(j))

    column(0, 0)
    column(0, 1)

    def start_tokens(j, unused):
        swap(j).start()
        load(j).start()
        return unused

    lax.fori_loop(0, chunks, start_tokens, 0)

    half = rows // 2
    ids = lax.broadcasted_iota(jnp.int32, (8, rows), 1)
    pos_mine[...] = jnp.where(ids < half, order_ref[0, 0], order_ref[0, 1]) * half + ids % half

    def pos_slot(device):
        return pos_all.at[:, pl.ds(pl.multiple_of(device * rows, rows), rows)]

    def pos_copy(d):
        return pltpu.make_async_remote_copy(
            pos_mine, pos_slot(ctx), pos_send.at[d], pos_recv.at[ctx],
            device_id=(z, (ctx + d) % plane), device_id_type=MESH,
        )

    for d in range(1, plane):
        pos_copy(d).start()
    pos_all[:, pl.ds(pl.multiple_of(ctx * rows, rows), rows)] = pos_mine[...]

    def wait_tokens(j, unused):
        load(j).wait()
        swap(j).wait()
        return unused

    lax.fori_loop(0, chunks, wait_tokens, 0)
    own_load.wait()
    acc[...] = jnp.dot(tok[own], w[own], preferred_element_type=jnp.float32)

    steps = dict(
        c=column, a=across, z=corner, C=finish_column, A=finish_across, Z=finish_corner
    )
    for kind, *where in order(layers):
        steps[kind](*where)

    total = pltpu.make_async_remote_copy(
        acc.at[pl.ds(rows, rows), :], share, sum_sem.at[0], sum_sem.at[1],
        device_id=(z, mate), device_id_type=MESH,
    )
    total.start()
    for conds, copy in sent:
        when(conds, lambda: copy().wait_send())
    for d in range(1, plane):
        pos_copy(d).wait_send()
        sender = (ctx + d) % plane
        pltpu.make_async_remote_copy(
            pos_mine, pos_slot(sender), pos_send.at[d], pos_recv.at[sender],
            device_id=(z, mate), device_id_type=MESH,
        ).wait_recv()
    pos_store = pltpu.make_async_copy(pos_all, pos_ref, store_sem.at[plane])
    pos_store.start()
    total.wait()
    mine[...] = (acc[0:rows, :] + share[...]).astype(jnp.bfloat16)

    part = rows // 2

    def block(device, first=0, size=rows):
        return gathered.at[pl.ds(pl.multiple_of(device * rows + first, part), size), :]

    lat_sent = []

    def lat_send_to(src, dst, recv, device):
        copy = pltpu.make_async_remote_copy(
            src, dst, lat_send.at[len(lat_sent)], lat_recv.at[recv], device_id=(z, device), device_id_type=MESH
        )
        copy.start()
        lat_sent.append(copy)

    def lat_arrived(dst, recv):
        pltpu.make_async_remote_copy(
            dst, dst, lat_send.at[0], lat_recv.at[recv], device_id=(z, mate), device_id_type=MESH
        ).wait_recv()

    stores = []

    def store(src, device, index):
        copy = pltpu.make_async_copy(
            src, latent_ref.at[pl.ds(pl.multiple_of(device * rows, rows), rows), :], store_sem.at[index]
        )
        copy.start()
        stores.append(copy)

    def partner(device):
        return device + 1 - 2 * core

    d_dev = pd * 2 + core
    low, high = pl.ds(0, part), pl.ds(part, part)
    lat_send_to(mine.at[low], block(ctx, 0, part), 0, x_dev)
    lat_send_to(mine.at[high], block(ctx, part, part), 1, y_dev)
    lat_send_to(mine.at[high], block(ctx, part, part), 9, x_dev)
    lat_send_to(mine.at[low], block(ctx, 0, part), 10, y_dev)
    lat_send_to(mine, block(ctx), 2, mate)
    store(mine, ctx, 0)
    lat_arrived(block(x_dev, 0, part), 0)
    lat_send_to(block(x_dev, 0, part), block(x_dev, 0, part), 3, y_dev)
    lat_arrived(block(y_dev, part, part), 1)
    lat_send_to(block(y_dev, part, part), block(y_dev, part, part), 4, x_dev)
    lat_arrived(block(x_dev, part, part), 9)
    lat_send_to(block(x_dev), block(x_dev), 5, mate)
    store(block(x_dev), x_dev, 1)
    lat_arrived(block(y_dev, 0, part), 10)
    lat_send_to(block(y_dev), block(y_dev), 6, mate)
    store(block(y_dev), y_dev, 2)
    lat_arrived(block(mate), 2)
    store(block(mate), mate, 3)
    lat_arrived(block(d_dev, 0, part), 3)
    lat_send_to(block(d_dev, 0, part), block(d_dev, 0, part), 7, mate)
    lat_arrived(block(d_dev, part, part), 4)
    lat_send_to(block(d_dev, part, part), block(d_dev, part, part), 8, mate)
    store(block(d_dev), d_dev, 4)
    lat_arrived(block(partner(x_dev)), 5)
    store(block(partner(x_dev)), partner(x_dev), 5)
    lat_arrived(block(partner(y_dev)), 6)
    store(block(partner(y_dev)), partner(y_dev), 6)
    lat_arrived(block(partner(d_dev), 0, part), 7)
    lat_arrived(block(partner(d_dev), part, part), 8)
    store(block(partner(d_dev)), partner(d_dev), 7)
    for copy in lat_sent:
        copy.wait_send()
    for copy in stores:
        copy.wait()
    pos_store.wait()


def gather_latent(layers, tokens, w_down, block_order):
    rows, features = tokens.shape[1], tokens.shape[2]
    depth, width = w_down.shape
    chunks = layers * 4
    dma = pltpu.SemaphoreType.DMA
    whole = pl.BlockSpec(memory_space=pltpu.HBM)
    return pl.pallas_call(
        functools.partial(latent_kernel, layers),
        out_shape=[
            jax.ShapeDtypeStruct((8 * rows, width), jnp.bfloat16),
            jax.ShapeDtypeStruct((8, 8 * rows), jnp.int32),
        ],
        in_specs=[pl.BlockSpec(memory_space=pltpu.SMEM), whole, whole],
        out_specs=[whole, whole],
        scratch_shapes=[
            pltpu.VMEM((chunks, 2 * rows, depth), jnp.bfloat16),
            pltpu.VMEM((chunks, depth, width), jnp.bfloat16),
            pltpu.VMEM((2 * rows, width), jnp.float32),
            pltpu.VMEM((rows, width), jnp.float32),
            pltpu.VMEM((rows, width), jnp.bfloat16),
            pltpu.VMEM((8 * rows, width), jnp.bfloat16),
            pltpu.VMEM((8, rows), jnp.int32),
            pltpu.VMEM((8, 8 * rows), jnp.int32),
            dma((chunks,)),
            dma,
            dma((chunks,)),
            dma((chunks,)),
            dma((160,)),
            dma((chunks, 2)),
            dma((layers, 4)),
            dma((8,)),
            dma((8,)),
            dma((2,)),
            dma((12,)),
            dma((11,)),
            dma((9,)),
        ],
        compiler_params=pltpu.CompilerParams(
            collective_id=0, has_side_effects=True, vmem_limit_bytes=48 * 2**20
        ),
        name="latent",
    )(block_order, tokens, w_down)


def per_device(layers, plane, tokens, w_down, w_up, queries, block_order):
    local_rows = tokens.shape[1]
    half_rows = local_rows // 2
    if plane == 8 and layers > 1:
        latent, positions = gather_latent(layers, tokens, w_down, block_order)
        return attend(block_order, positions, latent, w_up, queries)
    summed = jnp.dot(
        tokens[0],
        lax.all_gather(w_down, ("dp", "ctx"), axis=0, tiled=True),
        preferred_element_type=jnp.float32,
    )
    latent = lax.all_gather(summed.astype(jnp.bfloat16), "ctx", axis=0, tiled=True)
    order = lax.all_gather(block_order, "ctx", axis=1, tiled=True)
    positions = jnp.repeat(order, half_rows, axis=1) * half_rows + jnp.tile(
        jnp.arange(half_rows, dtype=jnp.int32), order.shape[1]
    )
    return attend(block_order, positions, latent, w_up, queries)


def solution(mesh):
    placed = (
        P("dp", "ctx", None),
        P(("dp", "ctx"), None),
        P(),
        P("dp", "ctx", None),
        P("dp", "ctx"),
    )
    sizes = mesh.shape["dp"], mesh.shape["ctx"]
    return jax.shard_map(
        functools.partial(per_device, *sizes), mesh=mesh, in_specs=placed, out_specs=P("dp", "ctx", None), check_vma=False
    )
```

```python
import functools
import math

import jax
import jax.numpy as jnp
from jax import lax
from jax.experimental import pallas as pl
from jax.experimental.pallas import tpu as pltpu
from jax.sharding import PartitionSpec as P

QH = 32
KVH = 4
HD = 128
MESH = pl.DeviceIdType.MESH


def attention_kernel(order_ref, pos_ref, latent_ref, w_up_ref, q_ref, out_ref, kv, bias):
    rows = q_ref.shape[1]
    count = latent_ref.shape[0]
    half = rows // 2
    tile = math.gcd(count, 256)

    @pl.loop(0, count // tile)
    def _(i):
        part = pl.ds(pl.multiple_of(i * tile, tile), tile)
        kv[part, :] = jnp.dot(
            latent_ref[part, :], w_up_ref[...], preferred_element_type=jnp.float32
        ).astype(jnp.bfloat16)

    ids = lax.broadcasted_iota(jnp.int32, (rows, 1), 0)
    query_pos = jnp.where(ids < half, order_ref[0, 0], order_ref[0, 1]) * half + ids % half
    bias[...] = jnp.where(pos_ref[0:1, :] <= query_pos, 0.0, -1e30)
    scale = HD ** (-0.5) * math.log2(math.e)
    heads = 2
    group = QH // KVH

    def cols(first, width):
        return pl.ds(pl.multiple_of(first * HD, HD), width * HD)

    def score(i):
        queries = jnp.concatenate(
            [q_ref[0, :, cols(i * heads + k, 1)] for k in range(heads)], axis=0
        )
        return lax.dot_general(
            queries,
            kv[:, cols(i * heads // group, 1)],
            (((1,), (1,)), ((), ())),
            preferred_element_type=jnp.float32,
        )

    def weigh(i, scores):
        parts, totals = [], []
        for first in range(0, heads * rows, strip):
            own = first % rows
            kept = scores[first : first + strip] * scale + bias[own : own + strip]
            largest = jnp.max(kept, axis=1, keepdims=True)
            expo = jnp.exp2(kept - largest)
            totals.append(jnp.sum(expo, axis=1, keepdims=True))
            parts.append(expo.astype(jnp.bfloat16))
        summed = jnp.dot(
            jnp.concatenate(parts, axis=0),
            kv[:, cols(KVH + i * heads // group, 1)],
            preferred_element_type=jnp.float32,
        )
        summed = (summed / jnp.concatenate(totals, axis=0)).astype(jnp.bfloat16)
        for k in range(heads):
            out_ref[0, :, cols(i * heads + k, 1)] = summed[k * rows : (k + 1) * rows]

    pairs = QH // heads
    together = 16 if count <= 1024 else 1
    strip = 16

    @pl.loop(0, pairs // together)
    def _(i):
        scores = score(i * together)
        for k in range(together):
            ahead = score(i * together + k + 1) if k + 1 < together else None
            weigh(i * together + k, scores)
            scores = ahead


def attend(block_order, positions, latent, w_up, queries):
    count = latent.shape[0]
    rows = queries.shape[1]
    vmem = pl.BlockSpec(memory_space=pltpu.VMEM)
    return pl.pallas_call(
        attention_kernel,
        out_shape=jax.ShapeDtypeStruct(queries.shape, jnp.bfloat16),
        in_specs=[pl.BlockSpec(memory_space=pltpu.SMEM), vmem, vmem, vmem, vmem],
        out_specs=vmem,
        scratch_shapes=[
            pltpu.VMEM((count, w_up.shape[1]), jnp.bfloat16),
            pltpu.VMEM((rows, count), jnp.float32),
        ],
        compiler_params=pltpu.CompilerParams(vmem_limit_bytes=48 * 2**20),
        name="attention",
    )(block_order, positions, latent, w_up, queries)


def order(layers):
    steps = [("a", 0, 0), ("c", 1, 0), ("a", 0, 1), ("c", 1, 1), ("z", 0, 0), ("z", 0, 1)]
    for t in range(1, layers):
        if t + 1 < layers:
            steps += [("c", t + 1, 0), ("c", t + 1, 1)]
        if t > 1:
            steps += [("z", t - 1, 0), ("z", t - 1, 1), ("A", t - 2)]
        steps += [("C", t), ("a", t, 0), ("a", t, 1)]
    steps += [("Z", t) for t in range(layers - 2)] + [("A", layers - 2)]
    steps += [("z", layers - 1, 0), ("z", layers - 1, 1), ("A", layers - 1), ("Z", layers - 2), ("Z", layers - 1)]
    return steps


def latent_kernel(
    layers, order_ref, tokens_ref, w_ref, latent_ref, pos_ref,
    tok, w, acc, share, mine, gathered, pos_mine, pos_all,
    load_sem, own_sem, tok_send, tok_recv, w_send, w_recv, piece_recv,
    pos_send, pos_recv, sum_sem, lat_send, lat_recv, store_sem,
):
    plane = 8
    z, ctx = lax.axis_index("dp"), lax.axis_index("ctx")
    core, x, y = ctx % 2, ctx // 2 % 2, ctx // 4
    mate = ctx + 1 - 2 * core
    x_dev, y_dev = ctx + 2 - 4 * x, ctx + 4 - 8 * y
    p, px, py = y * 2 + x, y * 2 + 1 - x, (1 - y) * 2 + x
    pd = (1 - y) * 2 + 1 - x
    rows, depth, width = tokens_ref.shape[1], w_ref.shape[0], w_ref.shape[1]
    chunks = layers * 4
    quarter = depth // 4
    own = z * 4 + p

    def columns(j, side):
        return pl.ds(pl.multiple_of((j * 2 + side) * depth, depth), depth)

    def load(j):
        return pltpu.make_async_copy(
            tokens_ref.at[0, :, columns(j, core)], tok.at[j, pl.ds(0, rows), :], load_sem.at[j]
        )

    def swap(j):
        return pltpu.make_async_remote_copy(
            tokens_ref.at[0, :, columns(j, 1 - core)], tok.at[j, pl.ds(rows, rows), :],
            tok_send.at[j], tok_recv.at[j], device_id=(z, mate), device_id_type=MESH,
        )

    own_load = pltpu.make_async_copy(w_ref, w.at[own], own_sem)
    own_load.start()

    barrier = pltpu.get_barrier_semaphore()
    for d in range(1, plane):
        pl.semaphore_signal(barrier, inc=1, device_id=(z, (ctx + d) % plane), device_id_type=MESH)

    @pl.when(z > 0)
    def _():
        pl.semaphore_signal(barrier, inc=1, device_id=(z - 1, ctx), device_id_type=MESH)

    @pl.when(z < layers - 1)
    def _():
        pl.semaphore_signal(barrier, inc=1, device_id=(z + 1, ctx), device_id_type=MESH)

    edge = layers - 1
    along = (z + edge - 1) // edge + (edge - z + edge - 1) // edge
    pl.semaphore_wait(barrier, plane - 1 + along)

    sent = []

    def send(conds, src, dst, sem, device):
        index = len(sent)

        def copy():
            return pltpu.make_async_remote_copy(
                src, dst, w_send.at[index], sem, device_id=device, device_id_type=MESH
            )

        sent.append((conds, copy))
        when(conds, lambda: copy().start())

    def when(conds, body):
        if not conds:
            body()
        elif len(conds) == 1:
            pl.when(conds[0])(body)
        else:
            pl.when(jnp.logical_and(conds[0], conds[1]))(body)

    def arrived(dst, sem):
        pltpu.make_async_remote_copy(
            dst, dst, w_send.at[0], sem, device_id=(z, mate), device_id_type=MESH
        ).wait_recv()

    def multiply(j):
        acc[...] += jnp.dot(tok[j], w[j], preferred_element_type=jnp.float32)

    def inside(layer):
        return jnp.logical_and(layer >= 0, layer < layers)

    def sources(t):
        if t == 0:
            return [(0, z, [])]
        return [(s, z + s * t, [inside(z + s * t)]) for s in (-1, 1)]

    def ahead(s):
        return [1, -1] if s == 0 else [-s]

    def piece(j, q):
        return w.at[j, pl.ds(q * quarter, quarter), :]

    def side(j, h):
        return w.at[j, pl.ds(h * 2 * quarter, 2 * quarter), :]

    def column(t, h):
        for s, layer, conds in sources(t):
            j = layer * 4 + p
            block = w_ref.at[pl.ds(h * 2 * quarter, 2 * quarter), :] if t == 0 else side(j, h)
            if t:
                when(conds, lambda: arrived(side(j, h), w_recv.at[j, h]))
            for step in ahead(s):
                send(conds + [inside(z + step)], block, side(j, h), w_recv.at[j, h], (z + step, ctx))
            for device in (x_dev, y_dev):
                send(conds, block, side(j, h), w_recv.at[j, h], (z, device))

    def across(t, h):
        place, device = ((px, y_dev), (py, x_dev))[h]
        for s, layer, conds in sources(t):
            j = layer * 4 + place
            when(conds, lambda: arrived(side(j, h), w_recv.at[j, h]))
            for q in (2 * h + 1, 2 * h) if t == 0 else (2 * h,):
                send(conds, piece(j, q), piece(j, q), piece_recv.at[layer, q], (z, device))

    def corner(t, h):
        q = 2 * h + 1
        for s, layer, conds in sources(t):
            j = layer * 4 + pd
            when(conds, lambda: arrived(piece(j, q), piece_recv.at[layer, q]))
            for step in ahead(s):
                send(
                    conds + [inside(z + step)], piece(j, q), piece(j, q), piece_recv.at[layer, q], (z + step, ctx)
                )

    def finish_column(t):
        for s, layer, conds in sources(t):
            when(conds, lambda: multiply(layer * 4 + p))

    def finish_across(t):
        for s, layer, conds in sources(t):
            for place, h in ((px, 1), (py, 0)):
                j = layer * 4 + place
                when(conds, lambda: arrived(side(j, h), w_recv.at[j, h]))
            for place in (px, py):
                when(conds, lambda: multiply(layer * 4 + place))

    def finish_corner(t):
        for s, layer, conds in sources(t):
            j = layer * 4 + pd
            for q in (0, 2):
                when(conds, lambda: arrived(piece(j, q), piece_recv.at[layer, q]))
            when(conds, lambda: multiply(j))

    column(0, 0)
    column(0, 1)

    def start_tokens(j, unused):
        swap(j).start()
        load(j).start()
        return unused

    lax.fori_loop(0, chunks, start_tokens, 0)

    half = rows // 2
    ids = lax.broadcasted_iota(jnp.int32, (8, rows), 1)
    pos_mine[...] = jnp.where(ids < half, order_ref[0, 0], order_ref[0, 1]) * half + ids % half

    def pos_slot(device):
        return pos_all.at[:, pl.ds(pl.multiple_of(device * rows, rows), rows)]

    def pos_copy(d):
        return pltpu.make_async_remote_copy(
            pos_mine, pos_slot(ctx), pos_send.at[d], pos_recv.at[ctx],
            device_id=(z, (ctx + d) % plane), device_id_type=MESH,
        )

    for d in range(1, plane):
        pos_copy(d).start()
    pos_all[:, pl.ds(pl.multiple_of(ctx * rows, rows), rows)] = pos_mine[...]

    def wait_tokens(j, unused):
        load(j).wait()
        swap(j).wait()
        return unused

    lax.fori_loop(0, chunks, wait_tokens, 0)
    own_load.wait()
    acc[...] = jnp.dot(tok[own], w[own], preferred_element_type=jnp.float32)

    steps = dict(
        c=column, a=across, z=corner, C=finish_column, A=finish_across, Z=finish_corner
    )
    for kind, *where in order(layers):
        steps[kind](*where)

    total = pltpu.make_async_remote_copy(
        acc.at[pl.ds(rows, rows), :], share, sum_sem.at[0], sum_sem.at[1],
        device_id=(z, mate), device_id_type=MESH,
    )
    total.start()
    for conds, copy in sent:
        when(conds, lambda: copy().wait_send())
    for d in range(1, plane):
        pos_copy(d).wait_send()
        sender = (ctx + d) % plane
        pltpu.make_async_remote_copy(
            pos_mine, pos_slot(sender), pos_send.at[d], pos_recv.at[sender],
            device_id=(z, mate), device_id_type=MESH,
        ).wait_recv()
    pos_store = pltpu.make_async_copy(pos_all, pos_ref, store_sem.at[plane])
    pos_store.start()
    total.wait()
    mine[...] = (acc[0:rows, :] + share[...]).astype(jnp.bfloat16)

    part = rows // 2

    def block(device, first=0, size=rows):
        return gathered.at[pl.ds(pl.multiple_of(device * rows + first, part), size), :]

    lat_sent = []

    def lat_send_to(src, dst, recv, device):
        copy = pltpu.make_async_remote_copy(
            src, dst, lat_send.at[len(lat_sent)], lat_recv.at[recv], device_id=(z, device), device_id_type=MESH
        )
        copy.start()
        lat_sent.append(copy)

    def lat_arrived(dst, recv):
        pltpu.make_async_remote_copy(
            dst, dst, lat_send.at[0], lat_recv.at[recv], device_id=(z, mate), device_id_type=MESH
        ).wait_recv()

    stores = []

    def store(src, device, index):
        copy = pltpu.make_async_copy(
            src, latent_ref.at[pl.ds(pl.multiple_of(device * rows, rows), rows), :], store_sem.at[index]
        )
        copy.start()
        stores.append(copy)

    def partner(device):
        return device + 1 - 2 * core

    d_dev = pd * 2 + core
    low, high = pl.ds(0, part), pl.ds(part, part)
    lat_send_to(mine.at[low], block(ctx, 0, part), 0, x_dev)
    lat_send_to(mine.at[high], block(ctx, part, part), 1, y_dev)
    lat_send_to(mine.at[high], block(ctx, part, part), 9, x_dev)
    lat_send_to(mine.at[low], block(ctx, 0, part), 10, y_dev)
    lat_send_to(mine, block(ctx), 2, mate)
    store(mine, ctx, 0)
    lat_arrived(block(x_dev, 0, part), 0)
    lat_send_to(block(x_dev, 0, part), block(x_dev, 0, part), 3, y_dev)
    lat_arrived(block(y_dev, part, part), 1)
    lat_send_to(block(y_dev, part, part), block(y_dev, part, part), 4, x_dev)
    lat_arrived(block(x_dev, part, part), 9)
    lat_send_to(block(x_dev), block(x_dev), 5, mate)
    store(block(x_dev), x_dev, 1)
    lat_arrived(block(y_dev, 0, part), 10)
    lat_send_to(block(y_dev), block(y_dev), 6, mate)
    store(block(y_dev), y_dev, 2)
    lat_arrived(block(mate), 2)
    store(block(mate), mate, 3)
    lat_arrived(block(d_dev, 0, part), 3)
    lat_send_to(block(d_dev, 0, part), block(d_dev, 0, part), 7, mate)
    lat_arrived(block(d_dev, part, part), 4)
    lat_send_to(block(d_dev, part, part), block(d_dev, part, part), 8, mate)
    store(block(d_dev), d_dev, 4)
    lat_arrived(block(partner(x_dev)), 5)
    store(block(partner(x_dev)), partner(x_dev), 5)
    lat_arrived(block(partner(y_dev)), 6)
    store(block(partner(y_dev)), partner(y_dev), 6)
    lat_arrived(block(partner(d_dev), 0, part), 7)
    lat_arrived(block(partner(d_dev), part, part), 8)
    store(block(partner(d_dev)), partner(d_dev), 7)
    for copy in lat_sent:
        copy.wait_send()
    for copy in stores:
        copy.wait()
    pos_store.wait()


def gather_latent(layers, tokens, w_down, block_order):
    rows, features = tokens.shape[1], tokens.shape[2]
    depth, width = w_down.shape
    chunks = layers * 4
    dma = pltpu.SemaphoreType.DMA
    whole = pl.BlockSpec(memory_space=pltpu.HBM)
    return pl.pallas_call(
        functools.partial(latent_kernel, layers),
        out_shape=[
            jax.ShapeDtypeStruct((8 * rows, width), jnp.bfloat16),
            jax.ShapeDtypeStruct((8, 8 * rows), jnp.int32),
        ],
        in_specs=[pl.BlockSpec(memory_space=pltpu.SMEM), whole, whole],
        out_specs=[whole, whole],
        scratch_shapes=[
            pltpu.VMEM((chunks, 2 * rows, depth), jnp.bfloat16),
            pltpu.VMEM((chunks, depth, width), jnp.bfloat16),
            pltpu.VMEM((2 * rows, width), jnp.float32),
            pltpu.VMEM((rows, width), jnp.float32),
            pltpu.VMEM((rows, width), jnp.bfloat16),
            pltpu.VMEM((8 * rows, width), jnp.bfloat16),
            pltpu.VMEM((8, rows), jnp.int32),
            pltpu.VMEM((8, 8 * rows), jnp.int32),
            dma((chunks,)),
            dma,
            dma((chunks,)),
            dma((chunks,)),
            dma((160,)),
            dma((chunks, 2)),
            dma((layers, 4)),
            dma((8,)),
            dma((8,)),
            dma((2,)),
            dma((12,)),
            dma((11,)),
            dma((9,)),
        ],
        compiler_params=pltpu.CompilerParams(
            collective_id=0, has_side_effects=True, vmem_limit_bytes=48 * 2**20
        ),
        name="latent",
    )(block_order, tokens, w_down)


def per_device(layers, plane, tokens, w_down, w_up, queries, block_order):
    local_rows = tokens.shape[1]
    half_rows = local_rows // 2
    if plane == 8 and layers > 1:
        latent, positions = gather_latent(layers, tokens, w_down, block_order)
        return attend(block_order, positions, latent, w_up, queries)
    summed = jnp.dot(
        tokens[0],
        lax.all_gather(w_down, ("dp", "ctx"), axis=0, tiled=True),
        preferred_element_type=jnp.float32,
    )
    latent = lax.all_gather(summed.astype(jnp.bfloat16), "ctx", axis=0, tiled=True)
    order = lax.all_gather(block_order, "ctx", axis=1, tiled=True)
    positions = jnp.repeat(order, half_rows, axis=1) * half_rows + jnp.tile(
        jnp.arange(half_rows, dtype=jnp.int32), order.shape[1]
    )
    return attend(block_order, positions, latent, w_up, queries)


def solution(mesh):
    placed = (
        P("dp", "ctx", None),
        P(("dp", "ctx"), None),
        P(),
        P("dp", "ctx", None),
        P("dp", "ctx"),
    )
    sizes = mesh.shape["dp"], mesh.shape["ctx"]
    return jax.shard_map(
        functools.partial(per_device, *sizes), mesh=mesh, in_specs=placed, out_specs=P("dp", "ctx", None), check_vma=False
    )
```

```python
import functools
import math

import jax
import jax.numpy as jnp
from jax import lax
from jax.experimental import pallas as pl
from jax.experimental.pallas import tpu as pltpu
from jax.sharding import PartitionSpec as P

QH = 32
KVH = 4
HD = 128
MESH = pl.DeviceIdType.MESH


def attention_kernel(order_ref, pos_ref, latent_ref, w_up_ref, q_ref, out_ref, kv, bias):
    rows = q_ref.shape[1]
    count = latent_ref.shape[0]
    half = rows // 2
    tile = math.gcd(count, 256)

    @pl.loop(0, count // tile)
    def _(i):
        part = pl.ds(pl.multiple_of(i * tile, tile), tile)
        kv[part, :] = jnp.dot(
            latent_ref[part, :], w_up_ref[...], preferred_element_type=jnp.float32
        ).astype(jnp.bfloat16)

    ids = lax.broadcasted_iota(jnp.int32, (rows, 1), 0)
    query_pos = jnp.where(ids < half, order_ref[0, 0], order_ref[0, 1]) * half + ids % half
    bias[...] = jnp.where(pos_ref[0:1, :] <= query_pos, 0.0, -1e30)
    scale = HD ** (-0.5) * math.log2(math.e)
    heads = 2
    group = QH // KVH

    def cols(first, width):
        return pl.ds(pl.multiple_of(first * HD, HD), width * HD)

    def score(i):
        queries = jnp.concatenate(
            [q_ref[0, :, cols(i * heads + k, 1)] for k in range(heads)], axis=0
        )
        return lax.dot_general(
            queries,
            kv[:, cols(i * heads // group, 1)],
            (((1,), (1,)), ((), ())),
            preferred_element_type=jnp.float32,
        )

    def weigh(i, scores):
        parts, totals = [], []
        for first in range(0, heads * rows, strip):
            own = first % rows
            kept = scores[first : first + strip] * scale + bias[own : own + strip]
            largest = jnp.max(kept, axis=1, keepdims=True)
            expo = jnp.exp2(kept - largest)
            totals.append(jnp.sum(expo, axis=1, keepdims=True))
            parts.append(expo.astype(jnp.bfloat16))
        summed = jnp.dot(
            jnp.concatenate(parts, axis=0),
            kv[:, cols(KVH + i * heads // group, 1)],
            preferred_element_type=jnp.float32,
        )
        summed = (summed / jnp.concatenate(totals, axis=0)).astype(jnp.bfloat16)
        for k in range(heads):
            out_ref[0, :, cols(i * heads + k, 1)] = summed[k * rows : (k + 1) * rows]

    pairs = QH // heads
    together = 16 if count <= 1024 else 1
    strip = 16

    @pl.loop(0, pairs // together)
    def _(i):
        scores = score(i * together)
        for k in range(together):
            ahead = score(i * together + k + 1) if k + 1 < together else None
            weigh(i * together + k, scores)
            scores = ahead


def attend(block_order, positions, latent, w_up, queries):
    count = latent.shape[0]
    rows = queries.shape[1]
    vmem = pl.BlockSpec(memory_space=pltpu.VMEM)
    return pl.pallas_call(
        attention_kernel,
        out_shape=jax.ShapeDtypeStruct(queries.shape, jnp.bfloat16),
        in_specs=[pl.BlockSpec(memory_space=pltpu.SMEM), vmem, vmem, vmem, vmem],
        out_specs=vmem,
        scratch_shapes=[
            pltpu.VMEM((count, w_up.shape[1]), jnp.bfloat16),
            pltpu.VMEM((rows, count), jnp.float32),
        ],
        compiler_params=pltpu.CompilerParams(vmem_limit_bytes=60 * 2**20),
        name="attention",
    )(block_order, positions, latent, w_up, queries)


def order(layers):
    steps = [("a", 0, 0), ("c", 1, 0), ("a", 0, 1), ("c", 1, 1), ("z", 0, 0), ("z", 0, 1)]
    for t in range(1, layers):
        if t + 1 < layers:
            steps += [("c", t + 1, 0), ("c", t + 1, 1)]
        if t > 1:
            steps += [("z", t - 1, 0), ("z", t - 1, 1), ("A", t - 2)]
        steps += [("C", t), ("a", t, 0), ("a", t, 1)]
    steps += [("Z", t) for t in range(layers - 2)] + [("A", layers - 2)]
    steps += [("z", layers - 1, 0), ("z", layers - 1, 1), ("A", layers - 1), ("Z", layers - 2), ("Z", layers - 1)]
    return steps


def latent_kernel(
    layers, order_ref, tokens_ref, w_ref, latent_ref, pos_ref,
    tok, w, acc, share, mine, gathered, pos_mine, pos_all,
    load_sem, own_sem, tok_send, tok_recv, w_send, w_recv, piece_recv,
    pos_send, pos_recv, sum_sem, lat_send, lat_recv, store_sem,
):
    plane = 8
    z, ctx = lax.axis_index("dp"), lax.axis_index("ctx")
    core, x, y = ctx % 2, ctx // 2 % 2, ctx // 4
    mate = ctx + 1 - 2 * core
    x_dev, y_dev = ctx + 2 - 4 * x, ctx + 4 - 8 * y
    p, px, py = y * 2 + x, y * 2 + 1 - x, (1 - y) * 2 + x
    pd = (1 - y) * 2 + 1 - x
    rows, depth, width = tokens_ref.shape[1], w_ref.shape[0], w_ref.shape[1]
    chunks = layers * 4
    quarter = depth // 4
    own = z * 4 + p

    def columns(j, side):
        return pl.ds(pl.multiple_of((j * 2 + side) * depth, depth), depth)

    def load(j):
        return pltpu.make_async_copy(
            tokens_ref.at[0, :, columns(j, core)], tok.at[j, pl.ds(0, rows), :], load_sem.at[j]
        )

    def swap(j):
        return pltpu.make_async_remote_copy(
            tokens_ref.at[0, :, columns(j, 1 - core)], tok.at[j, pl.ds(rows, rows), :],
            tok_send.at[j], tok_recv.at[j], device_id=(z, mate), device_id_type=MESH,
        )

    own_load = pltpu.make_async_copy(w_ref, w.at[own], own_sem)
    own_load.start()

    barrier = pltpu.get_barrier_semaphore()
    for d in range(1, plane):
        pl.semaphore_signal(barrier, inc=1, device_id=(z, (ctx + d) % plane), device_id_type=MESH)

    @pl.when(z > 0)
    def _():
        pl.semaphore_signal(barrier, inc=1, device_id=(z - 1, ctx), device_id_type=MESH)

    @pl.when(z < layers - 1)
    def _():
        pl.semaphore_signal(barrier, inc=1, device_id=(z + 1, ctx), device_id_type=MESH)

    edge = layers - 1
    along = (z + edge - 1) // edge + (edge - z + edge - 1) // edge
    pl.semaphore_wait(barrier, plane - 1 + along)

    sent = []

    def send(conds, src, dst, sem, device):
        index = len(sent)

        def copy():
            return pltpu.make_async_remote_copy(
                src, dst, w_send.at[index], sem, device_id=device, device_id_type=MESH
            )

        sent.append((conds, copy))
        when(conds, lambda: copy().start())

    def when(conds, body):
        if not conds:
            body()
        elif len(conds) == 1:
            pl.when(conds[0])(body)
        else:
            pl.when(jnp.logical_and(conds[0], conds[1]))(body)

    def arrived(dst, sem):
        pltpu.make_async_remote_copy(
            dst, dst, w_send.at[0], sem, device_id=(z, mate), device_id_type=MESH
        ).wait_recv()

    def multiply(j):
        acc[...] += jnp.dot(tok[j], w[j], preferred_element_type=jnp.float32)

    def inside(layer):
        return jnp.logical_and(layer >= 0, layer < layers)

    def sources(t):
        if t == 0:
            return [(0, z, [])]
        return [(s, z + s * t, [inside(z + s * t)]) for s in (-1, 1)]

    def ahead(s):
        return [1, -1] if s == 0 else [-s]

    def piece(j, q):
        return w.at[j, pl.ds(q * quarter, quarter), :]

    def side(j, h):
        return w.at[j, pl.ds(h * 2 * quarter, 2 * quarter), :]

    def column(t, h):
        for s, layer, conds in sources(t):
            j = layer * 4 + p
            block = w_ref.at[pl.ds(h * 2 * quarter, 2 * quarter), :] if t == 0 else side(j, h)
            if t:
                when(conds, lambda: arrived(side(j, h), w_recv.at[j, h]))
            for step in ahead(s):
                send(conds + [inside(z + step)], block, side(j, h), w_recv.at[j, h], (z + step, ctx))
            for device in (x_dev, y_dev):
                send(conds, block, side(j, h), w_recv.at[j, h], (z, device))

    def across(t, h):
        place, device = ((px, y_dev), (py, x_dev))[h]
        for s, layer, conds in sources(t):
            j = layer * 4 + place
            when(conds, lambda: arrived(side(j, h), w_recv.at[j, h]))
            for q in (2 * h + 1, 2 * h) if t == 0 else (2 * h,):
                send(conds, piece(j, q), piece(j, q), piece_recv.at[layer, q], (z, device))

    def corner(t, h):
        q = 2 * h + 1
        for s, layer, conds in sources(t):
            j = layer * 4 + pd
            when(conds, lambda: arrived(piece(j, q), piece_recv.at[layer, q]))
            for step in ahead(s):
                send(
                    conds + [inside(z + step)], piece(j, q), piece(j, q), piece_recv.at[layer, q], (z + step, ctx)
                )

    def finish_column(t):
        for s, layer, conds in sources(t):
            when(conds, lambda: multiply(layer * 4 + p))

    def finish_across(t):
        for s, layer, conds in sources(t):
            for place, h in ((px, 1), (py, 0)):
                j = layer * 4 + place
                when(conds, lambda: arrived(side(j, h), w_recv.at[j, h]))
            for place in (px, py):
                when(conds, lambda: multiply(layer * 4 + place))

    def finish_corner(t):
        for s, layer, conds in sources(t):
            j = layer * 4 + pd
            for q in (0, 2):
                when(conds, lambda: arrived(piece(j, q), piece_recv.at[layer, q]))
            when(conds, lambda: multiply(j))

    column(0, 0)
    column(0, 1)

    def start_tokens(j, unused):
        swap(j).start()
        load(j).start()
        return unused

    lax.fori_loop(0, chunks, start_tokens, 0)

    half = rows // 2
    ids = lax.broadcasted_iota(jnp.int32, (8, rows), 1)
    pos_mine[...] = jnp.where(ids < half, order_ref[0, 0], order_ref[0, 1]) * half + ids % half

    def pos_slot(device):
        return pos_all.at[:, pl.ds(pl.multiple_of(device * rows, rows), rows)]

    def pos_copy(d):
        return pltpu.make_async_remote_copy(
            pos_mine, pos_slot(ctx), pos_send.at[d], pos_recv.at[ctx],
            device_id=(z, (ctx + d) % plane), device_id_type=MESH,
        )

    for d in range(1, plane):
        pos_copy(d).start()
    pos_all[:, pl.ds(pl.multiple_of(ctx * rows, rows), rows)] = pos_mine[...]

    def wait_tokens(j, unused):
        load(j).wait()
        swap(j).wait()
        return unused

    lax.fori_loop(0, chunks, wait_tokens, 0)
    own_load.wait()
    acc[...] = jnp.dot(tok[own], w[own], preferred_element_type=jnp.float32)

    steps = dict(
        c=column, a=across, z=corner, C=finish_column, A=finish_across, Z=finish_corner
    )
    for kind, *where in order(layers):
        steps[kind](*where)

    total = pltpu.make_async_remote_copy(
        acc.at[pl.ds(rows, rows), :], share, sum_sem.at[0], sum_sem.at[1],
        device_id=(z, mate), device_id_type=MESH,
    )
    total.start()
    for conds, copy in sent:
        when(conds, lambda: copy().wait_send())
    for d in range(1, plane):
        pos_copy(d).wait_send()
        sender = (ctx + d) % plane
        pltpu.make_async_remote_copy(
            pos_mine, pos_slot(sender), pos_send.at[d], pos_recv.at[sender],
            device_id=(z, mate), device_id_type=MESH,
        ).wait_recv()
    pos_store = pltpu.make_async_copy(pos_all, pos_ref, store_sem.at[plane])
    pos_store.start()
    total.wait()
    mine[...] = (acc[0:rows, :] + share[...]).astype(jnp.bfloat16)

    part = rows // 2

    def block(device, first=0, size=rows):
        return gathered.at[pl.ds(pl.multiple_of(device * rows + first, part), size), :]

    lat_sent = []

    def lat_send_to(src, dst, recv, device):
        copy = pltpu.make_async_remote_copy(
            src, dst, lat_send.at[len(lat_sent)], lat_recv.at[recv], device_id=(z, device), device_id_type=MESH
        )
        copy.start()
        lat_sent.append(copy)

    def lat_arrived(dst, recv):
        pltpu.make_async_remote_copy(
            dst, dst, lat_send.at[0], lat_recv.at[recv], device_id=(z, mate), device_id_type=MESH
        ).wait_recv()

    stores = []

    def store(src, device, index):
        copy = pltpu.make_async_copy(
            src, latent_ref.at[pl.ds(pl.multiple_of(device * rows, rows), rows), :], store_sem.at[index]
        )
        copy.start()
        stores.append(copy)

    def partner(device):
        return device + 1 - 2 * core

    d_dev = pd * 2 + core
    low, high = pl.ds(0, part), pl.ds(part, part)
    lat_send_to(mine.at[low], block(ctx, 0, part), 0, x_dev)
    lat_send_to(mine.at[high], block(ctx, part, part), 1, y_dev)
    lat_send_to(mine.at[high], block(ctx, part, part), 9, x_dev)
    lat_send_to(mine.at[low], block(ctx, 0, part), 10, y_dev)
    lat_send_to(mine, block(ctx), 2, mate)
    store(mine, ctx, 0)
    lat_arrived(block(x_dev, 0, part), 0)
    lat_send_to(block(x_dev, 0, part), block(x_dev, 0, part), 3, y_dev)
    lat_arrived(block(y_dev, part, part), 1)
    lat_send_to(block(y_dev, part, part), block(y_dev, part, part), 4, x_dev)
    lat_arrived(block(x_dev, part, part), 9)
    lat_send_to(block(x_dev), block(x_dev), 5, mate)
    store(block(x_dev), x_dev, 1)
    lat_arrived(block(y_dev, 0, part), 10)
    lat_send_to(block(y_dev), block(y_dev), 6, mate)
    store(block(y_dev), y_dev, 2)
    lat_arrived(block(mate), 2)
    store(block(mate), mate, 3)
    lat_arrived(block(d_dev, 0, part), 3)
    lat_send_to(block(d_dev, 0, part), block(d_dev, 0, part), 7, mate)
    lat_arrived(block(d_dev, part, part), 4)
    lat_send_to(block(d_dev, part, part), block(d_dev, part, part), 8, mate)
    store(block(d_dev), d_dev, 4)
    lat_arrived(block(partner(x_dev)), 5)
    store(block(partner(x_dev)), partner(x_dev), 5)
    lat_arrived(block(partner(y_dev)), 6)
    store(block(partner(y_dev)), partner(y_dev), 6)
    lat_arrived(block(partner(d_dev), 0, part), 7)
    lat_arrived(block(partner(d_dev), part, part), 8)
    store(block(partner(d_dev)), partner(d_dev), 7)
    for copy in lat_sent:
        copy.wait_send()
    for copy in stores:
        copy.wait()
    pos_store.wait()


def gather_latent(layers, tokens, w_down, block_order):
    rows, features = tokens.shape[1], tokens.shape[2]
    depth, width = w_down.shape
    chunks = layers * 4
    dma = pltpu.SemaphoreType.DMA
    whole = pl.BlockSpec(memory_space=pltpu.HBM)
    return pl.pallas_call(
        functools.partial(latent_kernel, layers),
        out_shape=[
            jax.ShapeDtypeStruct((8 * rows, width), jnp.bfloat16),
            jax.ShapeDtypeStruct((8, 8 * rows), jnp.int32),
        ],
        in_specs=[pl.BlockSpec(memory_space=pltpu.SMEM), whole, whole],
        out_specs=[whole, whole],
        scratch_shapes=[
            pltpu.VMEM((chunks, 2 * rows, depth), jnp.bfloat16),
            pltpu.VMEM((chunks, depth, width), jnp.bfloat16),
            pltpu.VMEM((2 * rows, width), jnp.float32),
            pltpu.VMEM((rows, width), jnp.float32),
            pltpu.VMEM((rows, width), jnp.bfloat16),
            pltpu.VMEM((8 * rows, width), jnp.bfloat16),
            pltpu.VMEM((8, rows), jnp.int32),
            pltpu.VMEM((8, 8 * rows), jnp.int32),
            dma((chunks,)),
            dma,
            dma((chunks,)),
            dma((chunks,)),
            dma((160,)),
            dma((chunks, 2)),
            dma((layers, 4)),
            dma((8,)),
            dma((8,)),
            dma((2,)),
            dma((12,)),
            dma((11,)),
            dma((9,)),
        ],
        compiler_params=pltpu.CompilerParams(
            collective_id=0, has_side_effects=True, vmem_limit_bytes=60 * 2**20
        ),
        name="latent",
    )(block_order, tokens, w_down)


def per_device(layers, plane, tokens, w_down, w_up, queries, block_order):
    local_rows = tokens.shape[1]
    half_rows = local_rows // 2
    if plane == 8 and layers > 1:
        latent, positions = gather_latent(layers, tokens, w_down, block_order)
        return attend(block_order, positions, latent, w_up, queries)
    summed = jnp.dot(
        tokens[0],
        lax.all_gather(w_down, ("dp", "ctx"), axis=0, tiled=True),
        preferred_element_type=jnp.float32,
    )
    latent = lax.all_gather(summed.astype(jnp.bfloat16), "ctx", axis=0, tiled=True)
    order = lax.all_gather(block_order, "ctx", axis=1, tiled=True)
    positions = jnp.repeat(order, half_rows, axis=1) * half_rows + jnp.tile(
        jnp.arange(half_rows, dtype=jnp.int32), order.shape[1]
    )
    return attend(block_order, positions, latent, w_up, queries)


def solution(mesh):
    placed = (
        P("dp", "ctx", None),
        P(("dp", "ctx"), None),
        P(),
        P("dp", "ctx", None),
        P("dp", "ctx"),
    )
    sizes = mesh.shape["dp"], mesh.shape["ctx"]
    return jax.shard_map(
        functools.partial(per_device, *sizes), mesh=mesh, in_specs=placed, out_specs=P("dp", "ctx", None), check_vma=False
    )
```
